32 devices in a mesh: forest: 4 (over x, core), tile: 8 (over z, y).
Axes of the slice: x: 2, y: 2, z: 4, core: 2. Of those that a mesh axis runs over, the one named last changes fastest.
Arguments:
- left_panels: bfloat16 [4, 64, 2, 256, 256], P('forest', 'tile'), may hold values from -4 to 4
- right_panels: bfloat16 [4, 64, 1, 256, 256], P('forest', 'tile'), may hold values from -0.375 to 0.375
- dest_owner: int32 [4, 64, 1], P('forest', 'tile'), may hold values from 0 to 7; in each aligned block of 8 rows (0 to 7, 8 to 15, ..., all dimensions but the last counted through in order) at most 2 rows name the same one
- tile_slot: int32 [4, 64], P('forest', 'tile'), may hold values from 0 to 1
- frontal_tiles: float32 [16, 2, 256, 256], P('tile', None, 'forest'), may hold values from -6 to 6
- diag_inverse: float32 [256, 256], replicated, as said below
- reader_tile: int32 [32], replicated, may hold values from 0 to 15
Outputs:
- ancestor: float32 [16, 2, 256, 256], P('tile', None, 'forest')
- panel_read: float32 [32, 2, 256, 256], P('tile', None, 'forest')
The draws below stay inside these ranges and needn't reach their ends.
Inputs may be any that keep to these rules, and one draw needn't show every extreme that they name: `dest_owner`: among the pairs of one device at most 2 name the same owner, and some device has exactly 2 for one owner. `diag_inverse`: an upper triangular matrix with a positive diagonal.
All inputs are finite; a program needn't handle non-finite values.
Results may differ from the reference program's by a relative error of at most 0.0003.
Values may be sent and summed in bfloat16 or wider, within the bound.
No kernel may reach another device: no remote copies, remote signals or barrier semaphores. Data moves between devices by JAX's collectives and lax.ppermute only.
A program may use at most 192 MiB of HBM per device.

```python
import math
import jax
import jax.numpy as jnp
import numpy as np
from jax import lax

B = 256
R = 2
C = 1
PAIRS = 8
TILES_DEV = 2
READS = 4
CAP = 2
TILES = 16
N_FOREST = 4
N_TILE = 8


def draw_diag_inverse(key, part):
    key_off = jax.random.fold_in(key, 11)
    key_diag = jax.random.fold_in(key, 12)
    off_diagonal = jax.random.normal(key_off, (B, B), jnp.float32) * (0.5 / math.sqrt(B))
    diagonal = jax.random.uniform(key_diag, (B,), jnp.float32, 0.7, 1.4)
    return jnp.triu(off_diagonal, 1) + jnp.diag(diagonal)


def set_ends(result, rng, least, largest):
    spot = [jax.random.randint(jax.random.fold_in(rng, axis), (), 0, length) for axis, length in enumerate(result.shape)]
    main_axis = result.shape.index(max(result.shape))
    neighbour = spot[:main_axis] + [(spot[main_axis] + 1) % result.shape[main_axis]] + spot[main_axis + 1:]
    return result.at[tuple(spot)].set(least).at[tuple(neighbour)].set(largest)


def shard_levels(rng, shape, shards, least, largest):
    def one(axis_at, blocks):
        draws = jax.random.uniform(jax.random.fold_in(jax.random.fold_in(rng, 6), axis_at), (blocks,), jnp.float32, least / len(shards), largest / len(shards))
        return jnp.repeat(jnp.exp(draws), shape[axis_at] // blocks).reshape((-1,) + (1,) * (len(shape) - axis_at - 1))

    gain = one(*shards[0])
    for cut in shards[1:]:
        gain = gain * one(*cut)
    return gain


def assign_block(rng, own, number, rows, count, top, reach, skew):
    sequence = jax.random.permutation(rng, count)
    packed, ordinary = shares(count, rows * top, reach, skew, True), shares(count, rows * top, reach, skew, False)
    places = jnp.arange(count)

    def named(tallies, offset_by):
        used = int((tallies > 0).sum())
        fixed = max(1, used // 4)
        moved = fixed + (places - fixed + offset_by * (used - fixed)) % max(1, count - fixed)
        return jnp.zeros((count,), jnp.int32).at[sequence[jnp.where(places < fixed, places, moved)]].set(jnp.asarray(tallies, jnp.int32))

    tallies = jnp.where(number % 4 == 0, named(packed, number // 4), named(ordinary, number - number // 4 - 1))
    mixed = jax.random.permutation(jax.random.fold_in(own, 3), count)
    source_of, receiver = mixed[0:count // 2 * 2:2], mixed[1:count // 2 * 2:2]
    slack = jnp.minimum(tallies[source_of] - 1, reach - tallies[receiver]) // 2
    slack = jnp.where((source_of == sequence[0]) | (receiver == sequence[0]) | (tallies[receiver] == 0), 0, jnp.maximum(slack, 0))
    moved = jax.random.randint(jax.random.fold_in(own, 4), (count // 2,), 0, 1 << 20) % (slack + 1)
    tallies = tallies.at[source_of].add(-moved).at[receiver].add(moved)
    items = jnp.searchsorted(jnp.cumsum(tallies), jnp.arange(rows * top), side="right").astype(jnp.int32)
    grid = items.reshape(top, rows).T
    grid = grid[jax.random.permutation(jax.random.fold_in(own, 1), rows)]
    offset_by = jax.random.randint(jax.random.fold_in(own, 2), (rows, 1), 0, top)
    return jnp.take_along_axis(grid, (jnp.arange(top)[None, :] + offset_by) % top, axis=1)


def shares(number_of, total, reach, slope, full):
    weights = [(1 << 20) // math.isqrt(standing ** slope) + 1 for standing in range(1, number_of + 1)]
    largest = reach if full else min(reach, max(-(-total // number_of), total * weights[0] // sum(weights)))
    least = 1 if total - largest >= number_of - 1 else 0
    counts, spare = [largest] + [least] * (number_of - 1), total - largest - least * (number_of - 1)
    while spare > 0:
        free = [i for i in range(1, number_of) if counts[i] < largest] or [i for i in range(1, number_of) if counts[i] < reach]
        mass, budget = sum([weights[i] for i in free]), spare
        for i in free:
            extra = min(reach - counts[i], max(1, budget * weights[i] // mass), spare)
            counts[i] = counts[i] + extra
            spare = spare - extra
    return np.array(counts)


def normal_values(key, shape, deviation, reach, cuts=(), held_as=jnp.bfloat16):
    result = deviation * jax.random.normal(key, shape, jnp.float32)
    if cuts:
        result = result * shard_levels(key, shape, cuts, -0.22, 0.18)
    return jnp.clip(result, -reach, reach).astype(held_as)


def setup_inputs(seed: int = 0) -> dict:
    arg_keys = jax.random.split(jax.random.key(seed), 8)
    left_panels = normal_values(arg_keys[0], (N_FOREST, N_TILE * PAIRS, R, B, B), 0.25, 4.0, ((0, 4), (1, 8)))
    right_panels = normal_values(arg_keys[1], (N_FOREST, N_TILE * PAIRS, C, B, B), B ** -0.5, 0.375, ((0, 4), (1, 8)))
    dest_owner_keys = jax.random.split(jax.random.fold_in(arg_keys[2], 1), N_FOREST * (N_TILE * PAIRS) // PAIRS)
    dest_owner_turns = jax.random.permutation(jax.random.fold_in(arg_keys[2], 3), N_FOREST * (N_TILE * PAIRS) // PAIRS)
    dest_owner = jax.vmap(lambda own, number: assign_block(jax.random.fold_in(arg_keys[2], 2), own, number, PAIRS, N_TILE, 1, CAP, 2))(dest_owner_keys, dest_owner_turns).reshape((N_FOREST, N_TILE * PAIRS, 1))
    tile_slot = set_ends(jax.random.randint(arg_keys[3], (N_FOREST, N_TILE * PAIRS), 0, TILES_DEV), jax.random.fold_in(arg_keys[3], 1), 0, TILES_DEV - 1).astype(jnp.int32)
    frontal_tiles = normal_values(arg_keys[4], (TILES, R * C, B, B), 1.0, 6.0, ((0, 8), (2, 4)), jnp.float32)
    diag_inverse = draw_diag_inverse(jax.random.fold_in(arg_keys[7], 71), 0)
    reader_tile = set_ends(jax.random.randint(arg_keys[6], (N_TILE * READS,), 0, TILES), jax.random.fold_in(arg_keys[6], 1), 0, TILES - 1).astype(jnp.int32)
    return dict(left_panels=left_panels, right_panels=right_panels, dest_owner=dest_owner, tile_slot=tile_slot, frontal_tiles=frontal_tiles, diag_inverse=diag_inverse, reader_tile=reader_tile)


def reference(left_panels, right_panels, dest_owner, tile_slot, frontal_tiles, diag_inverse, reader_tile):
    tile_total = N_TILE * TILES_DEV

    def one_grid(running, grid_data):
        left_block, right_block, owners, slot_index = grid_data
        products = jnp.einsum("kaij,kcjl->kacil", left_block.astype(jnp.float32), right_block.astype(jnp.float32), precision=lax.Precision.HIGHEST)
        products = products.reshape(products.shape[0], R * C, B, B) / R
        target_tile = (owners[:, 0] * TILES_DEV + slot_index).astype(jnp.int32)
        return running.at[target_tile].add(products), None

    updates, _ = lax.scan(one_grid, jnp.zeros((tile_total, R * C, B, B), jnp.float32), (left_panels, right_panels, dest_owner, tile_slot))
    schur_tile = frontal_tiles - updates
    panel_tile = jnp.einsum("qtrj,jk->qtrk", schur_tile, diag_inverse, precision=lax.Precision.HIGHEST)
    return schur_tile, jnp.take(panel_tile, reader_tile.astype(jnp.int32), axis=0)
```

```python
import functools

import jax
import jax.numpy as jnp
from jax import lax
from jax.experimental import pallas as pl
from jax.experimental.pallas import tpu as pltpu
from jax.sharding import PartitionSpec as P

TOP = 32000.0
STEPS = 4.0
CORES = 2


def round_up(n, k):
    return -(-n // k) * k


def payload(n, half, width):
    return jax.ShapeDtypeStruct((n * half + round_up(n, 8), width), jnp.int32)


def encode(out_ref, i, n, tile):
    half = tile.shape[0] // 2
    largest = jnp.max(jnp.abs(tile), axis=0, keepdims=True)
    level = jnp.ceil(jnp.log2(jnp.maximum(largest, 1e-30)) * STEPS)
    out_ref[pl.ds(n * half + i, 1), :] = level.astype(jnp.int32)
    code = (tile * (jnp.exp2(level * (-1.0 / STEPS)) * TOP) + 32768.5).astype(jnp.int32)
    out_ref[pl.ds(i * half, half), :] = (code[:half] << 16) | code[half:]


def decode(ref, i, n, half):
    level = ref[pl.ds(n * half + i, 1), :].astype(jnp.float32)
    scale = jnp.exp2(level * (1.0 / STEPS)) * (1.0 / TOP)
    codes = ref[pl.ds(i * half, half), :]
    high = lax.shift_right_logical(codes, 16).astype(jnp.float32) - 32768.0
    low = (codes & 0xFFFF).astype(jnp.float32) - 32768.0
    return jnp.concatenate([high * scale, low * scale], axis=0)


def loop(n, body):
    if n <= 32:
        for i in range(n):
            body(i)
    else:

        def step(i, carry):
            body(i)
            return carry

        lax.fori_loop(0, n, step, 0)


def split(read, keep_ref, out_refs, digit, pre, size, post):
    n = pre * post

    def index(i, d):
        return ((i // post) * size + d) * post + i % post

    for j, out_ref in enumerate(out_refs, 1):
        other = lax.rem(digit + j, size)
        loop(n, lambda i: encode(out_ref, i, n, read(index(i, other))))

    def keep(i):
        keep_ref[i] = read(index(i, digit))

    loop(n, keep)


def digits(cores, ys):
    f, t = lax.axis_index("forest"), lax.axis_index("tile")
    return {"core": lax.rem(f, cores), "x": f // cores, "y": lax.rem(t, ys), "z": t // ys}


def multiply_kernel(where, target, other, left, right, left2, right2, *rest, plan):
    outs, acc = rest[:-1], rest[-1]
    axis, pre, size, post, ys = plan
    per = acc.shape[0] // plan_groups(acc, left, right)
    acc[...] = jnp.zeros_like(acc)
    for names, l_ref, r_ref in ((target, left, right), (other, left2, right2)):
        for k in range(r_ref.shape[0]):
            blocks, xs, _, rows, width = l_ref.shape[1:]
            lhs = l_ref[k].reshape(blocks * xs * rows, width)
            for c in range(r_ref.shape[1]):
                product = jnp.dot(lhs, r_ref[k, c], preferred_element_type=jnp.float32)
                product = product.reshape(blocks, xs, rows, r_ref.shape[3])
                for a in range(blocks):
                    at = names[k] * per + (a * r_ref.shape[1] + c) * xs
                    acc[pl.ds(at, xs)] += product[a]
    digit = digits(CORES, ys)[axis]
    split(lambda i: acc[i], outs[0], outs[1:], digit, pre, size, post)


def plan_groups(acc, left, right):
    return acc.shape[0] // (left.shape[1] * left.shape[2] * right.shape[1])


def pass_kernel(*refs, plan):
    axis, received, pre, size, post, ys = plan
    kept, come = refs[0], refs[1 : 1 + received]
    outs = refs[1 + received :]
    n, rows = kept.shape[0], kept.shape[1]

    def read(i):
        tile = kept[i]
        for ref in come:
            tile = tile + decode(ref, i, n, rows // 2)
        return tile

    split(read, outs[0], outs[1:], digits(CORES, ys)[axis], pre, size, post)


def solve_kernel(*refs, received, depth):
    kept, come = refs[0], refs[1 : 1 + received]
    frontal, inverse, schur, out = refs[1 + received :]
    n, rows = kept.shape[0], kept.shape[1]
    for i in range(n):
        tile = kept[i]
        for ref in come:
            tile = tile + decode(ref, i, n, rows // 2)
        tile = frontal[i] - tile / depth
        schur[i] = tile
        panel = jnp.dot(tile, inverse[...], precision=lax.Precision.HIGHEST, preferred_element_type=jnp.float32)
        encode(out, i, n, panel)


def owner_of(group, per_dev, ys):
    t = group // per_dev
    return t // ys, lax.rem(t, ys), lax.rem(group, per_dev)


def pick_kernel(reader, *refs, zs, ys, per_dev, tiles, reads, half):
    sources, outs = refs[:zs], refs[zs:]
    at = digits(CORES, ys)
    n_in, n_out = per_dev * tiles, reads * tiles
    for j, out in enumerate(outs, 1):
        to = lax.rem(at["y"] + j, ys)
        for i in range(reads):
            z, y, slot = owner_of(reader[(at["z"] * ys + to) * reads + i], per_dev, ys)
            back = lax.rem(at["z"] - z + zs, zs)
            for b in range(zs):

                @pl.when((y == at["y"]) & (back == b))
                def _():
                    for a in range(tiles):
                        k, o = slot * tiles + a, i * tiles + a
                        out[pl.ds(o * half, half), :] = sources[b][pl.ds(pl.multiple_of(k * half, half), half), :]
                        out[pl.ds(n_out * half + o, 1), :] = sources[b][pl.ds(n_in * half + k, 1), :]


def read_kernel(reader, *refs, zs, ys, per_dev, tiles, reads, half, streams):
    out = refs[-1]
    at = digits(CORES, ys)
    n_in, n_out = per_dev * tiles, reads * tiles
    for i in range(reads):
        z, y, slot = owner_of(reader[(at["z"] * ys + at["y"]) * reads + i], per_dev, ys)
        back = lax.rem(at["z"] - z + zs, zs)
        back_y = lax.rem(at["y"] - y + ys, ys)
        for s in range(streams):
            mine = refs[s * (zs + ys - 1) : (s + 1) * (zs + ys - 1)]
            for b in range(zs):

                @pl.when((back_y == 0) & (back == b))
                def _():
                    for a in range(tiles):
                        k = slot * tiles + a
                        out[i, s * tiles + a] = decode_at(mine[b], k, n_in, half)

            for b in range(1, ys):

                @pl.when(back_y == b)
                def _():
                    for a in range(tiles):
                        out[i, s * tiles + a] = decode(mine[zs + b - 1], i * tiles + a, n_out, half)


def decode_at(ref, i, n, half):
    level = ref[pl.ds(n * half + i, 1), :].astype(jnp.float32)
    scale = jnp.exp2(level * (1.0 / STEPS)) * (1.0 / TOP)
    codes = ref[pl.ds(pl.multiple_of(i * half, half), half), :]
    high = lax.shift_right_logical(codes, 16).astype(jnp.float32) - 32768.0
    low = (codes & 0xFFFF).astype(jnp.float32) - 32768.0
    return jnp.concatenate([high * scale, low * scale], axis=0)


def per_device(
    left_panels, right_panels, dest_owner, tile_slot, frontal_tiles, diag_inverse, reader_tile, *, ys
):
    forests, owners = lax.axis_size("forest"), lax.axis_size("tile")
    xs, zs = forests // CORES, owners // ys
    _, pairs, left_depth, block, width = left_panels.shape
    right_depth = right_panels.shape[2]
    columns = right_panels.shape[4]
    per_dev, tile_depth, rows, _ = frontal_tiles.shape
    half = rows // 2
    groups = owners * per_dev
    reads = reader_tile.shape[0] // owners
    core = lax.rem(lax.axis_index("forest"), CORES)

    def shift(value, axis, j):
        if axis in ("x", "core"):
            perm = [
                (x * CORES + c, ((x + j) % xs) * CORES + c) if axis == "x" else (x * CORES + c, x * CORES + (c + j) % CORES)
                for x in range(xs)
                for c in range(CORES)
            ]
            return lax.ppermute(value, "forest", perm)
        perm = [
            (z * ys + y, ((z + j) % zs) * ys + y) if axis == "z" else (z * ys + y, z * ys + (y + j) % ys)
            for z in range(zs)
            for y in range(ys)
        ]
        return lax.ppermute(value, "tile", perm)

    def spread(values, axis):
        return [shift(v, axis, j) for j, v in enumerate(values, 1)]

    def call(kernel, shapes, args, scratch=(), smem=0, specs=None):
        whole = pl.BlockSpec(memory_space=pltpu.VMEM)
        return pl.pallas_call(
            kernel,
            out_shape=shapes,
            in_specs=specs or [pl.BlockSpec(memory_space=pltpu.SMEM)] * smem + [whole] * (len(args) - smem),
            out_specs=[whole] * len(shapes) if isinstance(shapes, list) else whole,
            scratch_shapes=scratch,
        )(*args)

    def kept(n):
        return jax.ShapeDtypeStruct((n, rows, columns), jnp.float32)

    left = left_panels.reshape(pairs, left_depth, xs, CORES, rows, width)
    right = right_panels.reshape(pairs, right_depth, width, columns)
    target = (dest_owner[0, :, 0] * per_dev + tile_slot[0]).astype(jnp.int32)
    where = jnp.reshape(core, (1,)).astype(jnp.int32)
    right2 = shift(right, "core", 1)
    other = shift(target, "core", 1)
    parts = 2
    blocks = left_depth // parts
    tiles = blocks * right_depth
    sizes = {"x": xs, "y": ys, "z": zs}

    def multiply(s, axis, pre, post):
        mine = left[:, s * blocks : (s + 1) * blocks]
        sent = lax.dynamic_slice_in_dim(mine, (core + 1) % CORES, 1, 3)
        left2 = shift(sent, "core", 1)
        n = groups * tiles * xs
        size = sizes[axis]
        one = (pairs, blocks, xs, 1, rows, width)
        full = lambda shape: pl.BlockSpec(shape, lambda i, *_: (0,) * len(shape))
        outs = [kept(n // size)] + [payload(n // size, half, columns)] * (size - 1)
        return pl.pallas_call(
            functools.partial(multiply_kernel, plan=(axis, pre, size, post, ys)),
            out_shape=outs,
            grid_spec=pltpu.PrefetchScalarGridSpec(
                num_scalar_prefetch=3,
                grid=(1,),
                in_specs=[
                    pl.BlockSpec(one, lambda i, w, *_: (0, s, 0, w[0], 0, 0)),
                    full(right.shape),
                    full(one),
                    full(right.shape),
                ],
                out_specs=[full(o.shape) for o in outs],
                scratch_shapes=[pltpu.VMEM((n, rows, columns), jnp.float32)],
            ),
        )(where, target, other, left, right, left2, right2)

    def passed(state, axis, pre, post):
        keep, come = state
        size = sizes[axis]
        n = keep.shape[0] // size
        out = call(
            functools.partial(pass_kernel, plan=(axis, len(come), pre, size, post, ys)),
            [kept(n)] + [payload(n, half, columns)] * (size - 1),
            [keep, *come],
        )
        return out[0], spread(out[1:], axis)

    states = []
    first = multiply(0, "x", groups * tiles, 1)
    second = multiply(1, "y", zs, per_dev * tiles * xs)
    states = [(first[0], spread(first[1:], "x")), (second[0], spread(second[1:], "y"))]
    states = [passed(states[0], "y", zs, per_dev * tiles), passed(states[1], "x", zs * per_dev * tiles, 1)]
    states = [passed(s, "z", 1, per_dev * tiles) for s in states]

    schur, pieces = [], []
    for s, (keep, come) in enumerate(states):
        frontal = frontal_tiles[:, s * tiles : (s + 1) * tiles].reshape(per_dev * tiles, rows, columns)
        n = per_dev * tiles
        solved, panel = call(
            functools.partial(solve_kernel, received=len(come), depth=float(left_depth)),
            [kept(n), payload(n, half, columns)],
            [keep, *come, frontal, diag_inverse],
        )
        schur.append(solved.reshape(per_dev, tiles, rows, columns))
        along = [panel] + spread([panel] * (zs - 1), "z")
        picked = call(
            functools.partial(
                pick_kernel, zs=zs, ys=ys, per_dev=per_dev, tiles=tiles, reads=reads, half=half
            ),
            [payload(reads * tiles, half, columns)] * (ys - 1),
            [reader_tile, *along],
            smem=1,
        )
        pieces += along + spread(picked, "y")
    out = call(
        functools.partial(
            read_kernel, zs=zs, ys=ys, per_dev=per_dev, tiles=tiles, reads=reads, half=half, streams=parts
        ),
        jax.ShapeDtypeStruct((reads, tile_depth, rows, columns), jnp.float32),
        [reader_tile, *pieces],
        smem=1,
    )
    return jnp.concatenate(schur, axis=1), out


def tile_rows(mesh):
    line = mesh.devices[0]
    places = [getattr(d, "coords", None) for d in line]
    if any(p is None for p in places):
        return mesh.shape["forest"] // CORES
    count = 1
    while count < len(line) and places[count][2] == places[0][2]:
        count += 1
    return count


def solution(mesh):
    placed = (
        P("forest", "tile", None, None, None),
        P("forest", "tile", None, None, None),
        P("forest", "tile", None),
        P("forest", "tile"),
        P("tile", None, "forest", None),
        P(),
        P(),
    )
    return jax.shard_map(
        functools.partial(per_device, ys=tile_rows(mesh)),
        mesh=mesh,
        in_specs=placed,
        out_specs=(P("tile", None, "forest", None), P("tile", None, "forest", None)),
        check_vma=False,
    )
```

```python
import functools

import jax
import jax.numpy as jnp
from jax import lax
from jax.experimental import pallas as pl
from jax.experimental.pallas import tpu as pltpu
from jax.sharding import PartitionSpec as P

TOP = 32000.0
STEPS = 4.0
CORES = 2
STREAMS = 3
VMEM = pltpu.MemorySpace.VMEM


def code_rows(depth, rows):
    return depth // 2 * rows


def payload_rows(n, depth, rows):
    return n * code_rows(depth, rows) + -(-n // 8) * 8


def encode(out, base, i, n, tile):
    depth, rows, _ = tile.shape
    size = code_rows(depth, rows)
    largest = jnp.max(jnp.max(jnp.abs(tile), axis=0), axis=0, keepdims=True)
    level = jnp.ceil(jnp.log2(jnp.maximum(largest, 1e-30)) * STEPS)
    out[pl.ds(base + n * size + i, 1), :] = level.astype(jnp.int32)
    code = (tile * (jnp.exp2(level * (-1.0 / STEPS)) * TOP)[None] + 32768.5).astype(jnp.int32)
    for q in range(depth // 2):
        at = base + i * size + q * rows
        out[pl.ds(pl.multiple_of(at, 8), rows), :] = (code[2 * q] << 16) | code[2 * q + 1]


def decode(ref, base, i, n, depth, rows):
    size = code_rows(depth, rows)
    level = ref[pl.ds(base + n * size + i, 1), :].astype(jnp.float32)
    scale = jnp.exp2(level * (1.0 / STEPS)) * (1.0 / TOP)
    blocks = []
    for q in range(depth // 2):
        codes = ref[pl.ds(pl.multiple_of(base + i * size + q * rows, 8), rows), :]
        blocks.append((lax.shift_right_logical(codes, 16).astype(jnp.float32) - 32768.0) * scale)
        blocks.append(((codes & 0xFFFF).astype(jnp.float32) - 32768.0) * scale)
    return jnp.stack(blocks)


def loop(n, body):
    if n <= 16:
        for i in range(n):
            body(i)
    else:

        def step(i, carry):
            body(i)
            return carry

        lax.fori_loop(0, n, step, 0)


def bit(axis, b, ys):
    f, t = lax.axis_index("forest"), lax.axis_index("tile")
    place = {"x": f // CORES, "y": lax.rem(t, ys), "z": t // ys}[axis]
    return lax.rem(lax.shift_right_logical(place, b), 2)


def fetch_kernel(*refs, other, plain):
    left, sem, outs = refs[0], refs[-1], refs[1 + plain : -1]
    core = lax.rem(lax.axis_index("forest"), CORES)
    core = CORES - 1 - core if other else core
    copies = [
        pltpu.make_async_copy(left.at[:, a, :, core], outs[0].at[:, :, a], sem.at[a]) for a in range(left.shape[1])
    ]
    for i in range(plain):
        copies.append(pltpu.make_async_copy(refs[1 + i], outs[1 + i], sem.at[left.shape[1] + i]))
    for c in copies:
        c.start()
    for c in copies:
        c.wait()


def multiply_kernel(owner, slot, left, right, *rest, per_dev):
    acc = rest[-1]
    if len(rest) == 1:
        acc[...] = jnp.zeros_like(acc)
    pairs, xs, blocks, rows, width = left.shape
    for k in range(pairs):
        lhs = left[k].reshape(xs * blocks * rows, width)
        at = (owner[k] * per_dev + slot[k]) * xs
        for c in range(right.shape[1]):
            product = jnp.dot(lhs, right[k, c], preferred_element_type=jnp.float32)
            product = product.reshape(xs, blocks, rows, right.shape[3])
            for a in range(blocks):
                acc[pl.ds(at, xs), a * right.shape[1] + c] += product[:, a]


def half_kernel(*refs, span, pre, post, axis, b, ys, send):
    kept, come, out = refs[0], refs[1:-1], refs[-1]
    n, depth = 2 * pre * post, kept.shape[1]
    digit = bit(axis, b, ys)
    digit = 1 - digit if send else digit

    def body(i):
        at = ((i // post) * 2 + digit) * post + i % post
        tile = kept[at, :, span[0] : span[1], :]
        for ref in come:
            tile = tile + decode(ref, 0, at, n, depth, span[1] - span[0])
        if send:
            encode(out, 0, i, n // 2, tile)
        else:
            out[i] = tile

    loop(pre * post, body)


def share_kernel(*refs, depth, span, axis, b, ys):
    kept, come = refs[0], refs[1:-3]
    frontal, part, out = refs[-3:]
    n, blocks, rows, _ = kept.shape
    per_dev = n // 2
    digit = bit(axis, b, ys)
    for d in range(2):
        owned = (digit == d).astype(jnp.float32)
        for k in range(per_dev):
            i = d * per_dev + k
            tile = kept[i]
            for ref in come:
                tile = tile + decode(ref, 0, i, n, blocks, rows)
            tile = frontal[k, :, span[0] : span[1], :] * owned - tile * (1.0 / depth)
            part[i] = tile
            encode(out, 0, i, n, tile)


def solve_kernel(part, come, inverse, schur, out, whole, *, axis, b, ys):
    n, blocks, rows, columns = part.shape
    per_dev = n // 2
    for i in range(n):
        whole[i] = part[i] + decode(come, 0, i, n, blocks, rows)
    schur[...] = whole[pl.ds(bit(axis, b, ys) * per_dev, per_dev)]
    full = whole[...].reshape(n * blocks * rows, columns)
    panel = jnp.dot(full, inverse[...], precision=lax.Precision.HIGHEST, preferred_element_type=jnp.float32)
    panel = panel.reshape(n, blocks, rows, inverse.shape[1])
    for i in range(n):
        encode(out, 0, i, n, panel[i])


def join_kernel(*refs):
    out, at = refs[-1], 0
    for ref in refs[:-1]:
        out[at : at + ref.shape[0], :] = ref[...]
        at += ref.shape[0]


def schur_kernel(*refs, spans):
    for ref, (low, high) in zip(refs[:-1], spans):
        refs[-1][:, :, low:high, :] = ref[...]


def locate(group, per_dev, ys, top, bits):
    t = group // per_dev
    z = t // ys
    apart = lax.bitwise_xor(z, lax.axis_index("tile") // ys)
    at = 0
    for i, b in enumerate(bits):
        at = at + lax.rem(lax.shift_right_logical(apart, b), 2) * (1 << i)
    tile = lax.rem(lax.shift_right_logical(z, top), 2) * per_dev + lax.rem(group, per_dev)
    return lax.rem(t, ys), tile, at


def pick_kernel(reader, *refs, outs, ys, top, bits, per_dev, reads, depth, rows):
    spread, outs = refs[:-outs], refs[-outs:]
    t = lax.axis_index("tile")
    z, y = t // ys, lax.rem(t, ys)
    size, each = code_rows(depth, rows), payload_rows(2 * per_dev, depth, rows)
    share = (1 << len(bits)) // len(spread)
    for j, out in enumerate(outs, 1):
        to = lax.bitwise_xor(y, j)
        for i in range(reads):
            owner, tile, at = locate(reader[(z * ys + to) * reads + i], per_dev, ys, top, bits)
            for h, ref in enumerate(spread):

                @pl.when((owner == y) & (at // share == h))
                def _():
                    base = lax.rem(at, share) * each
                    out[i * size : (i + 1) * size, :] = ref[pl.ds(pl.multiple_of(base + tile * size, 8), size), :]
                    out[reads * size + i : reads * size + i + 1, :] = ref[pl.ds(base + 2 * per_dev * size + tile, 1), :]


def read_kernel(reader, *refs, ys, top, bits, per_dev, reads, depth, span, many):
    inputs, (out, buf, sem) = refs[:many], refs[-3:]
    t = lax.axis_index("tile")
    z, y = t // ys, lax.rem(t, ys)
    spread, picked = inputs[: many - (ys - 1)], inputs[many - (ys - 1) :]
    rows = span[1] - span[0]
    each = payload_rows(2 * per_dev, depth, rows)
    share = (1 << len(bits)) // len(spread)
    copies = []
    for i in range(reads):
        owner, tile, at = locate(reader[(z * ys + y) * reads + i], per_dev, ys, top, bits)
        apart = lax.bitwise_xor(owner, y)
        for h, ref in enumerate(spread):

            @pl.when((apart == 0) & (at // share == h))
            def _():
                base = lax.rem(at, share) * each
                buf[i] = decode(ref, base, tile, 2 * per_dev, depth, rows)

        for j, ref in enumerate(picked, 1):

            @pl.when(apart == j)
            def _():
                buf[i] = decode(ref, 0, i, reads, depth, rows)

        copies.append(pltpu.make_async_copy(buf.at[i], out.at[i, :, span[0] : span[1], :], sem.at[i]))
        copies[-1].start()
    for c in copies:
        c.wait()


def per_device(
    left_panels, right_panels, dest_owner, tile_slot, frontal_tiles, diag_inverse, reader_tile, *, ys
):
    forests, owners = lax.axis_size("forest"), lax.axis_size("tile")
    xs, zs = forests // CORES, owners // ys
    _, pairs, left_depth, _, width = left_panels.shape
    columns = right_panels.shape[4]
    per_dev, depth, rows, _ = frontal_tiles.shape
    groups = owners * per_dev
    reads = reader_tile.shape[0] // owners

    def partner(value, axis, j):
        if axis in ("x", "core"):
            step = j if axis == "core" else j * CORES
            return lax.ppermute(value, "forest", [(f, f ^ step) for f in range(forests)])
        step = j if axis == "y" else j * ys
        return lax.ppermute(value, "tile", [(t, t ^ step) for t in range(owners)])

    def near(value):
        return pltpu.with_memory_space_constraint(value, VMEM)

    def call(kernel, shapes, args, smem=0, scratch=(), aliases={}, specs=None, room=4 << 20):
        near_spec = pl.BlockSpec(memory_space=pltpu.VMEM)
        small = pl.BlockSpec(memory_space=pltpu.SMEM)
        return pl.pallas_call(
            kernel,
            out_shape=shapes,
            in_specs=[small] * smem + [near_spec] * (len(args) - smem),
            out_specs=[near_spec] * len(shapes),
            scratch_shapes=scratch,
            input_output_aliases=aliases,
            compiler_params=pltpu.CompilerParams(vmem_limit_bytes=room),
        )(*args[:smem], *map(near, args[smem:]))

    def coded(n, r):
        return pltpu.VMEM((payload_rows(n, depth, r), columns), jnp.int32)

    def floats(n, r):
        return pltpu.VMEM((n, depth, r, columns), jnp.float32)

    left = left_panels.reshape(pairs, left_depth, xs, CORES, rows, width)
    right = right_panels[0]
    owner, slot = dest_owner[0, :, 0], tile_slot[0]
    right2 = partner(right, "core", 1)
    owner2, slot2 = partner(owner, "core", 1), partner(slot, "core", 1)

    def fetch(other, plain):
        half = pltpu.VMEM((pairs, xs, left_depth, rows, width), left.dtype)
        shapes = [half] + [pltpu.VMEM(p.shape, p.dtype) for p in plain]
        return pl.pallas_call(
            functools.partial(fetch_kernel, other=other, plain=len(plain)),
            out_shape=shapes,
            in_specs=[pl.BlockSpec(memory_space=pltpu.HBM)] * (1 + len(plain)),
            out_specs=[pl.BlockSpec(memory_space=pltpu.VMEM)] * len(shapes),
            scratch_shapes=[pltpu.SemaphoreType.DMA((left_depth + len(plain),))],
            compiler_params=pltpu.CompilerParams(vmem_limit_bytes=1 << 20),
        )(*[pltpu.with_memory_space_constraint(v, pltpu.MemorySpace.HBM) for v in (left, *plain)])

    (sent,) = fetch(True, [])
    left2 = partner(sent, "core", 1)
    mine, right = fetch(False, [right])
    acc_shape = [floats(groups * xs, rows)]
    multiply = functools.partial(multiply_kernel, per_dev=per_dev)
    (acc,) = call(multiply, acc_shape, [owner, slot, mine, right], smem=2)
    (acc,) = call(multiply, acc_shape, [owner2, slot2, left2, right2, acc], smem=2, aliases={4: 0})

    def bits_of(axis, size):
        return [(axis, b) for b in range(size.bit_length() - 1)]

    x, y, z = bits_of("x", xs), bits_of("y", ys), bits_of("z", zs)
    top, low = z[-1], z[:-1]
    orders = [x + y + low, y + low[:1] + x + low[1:], low[:1] + x + y + low[1:]]
    units = rows // 8
    ends = [0]
    for s in range(STREAMS):
        ends.append(ends[-1] + (units + STREAMS - 1 - s) // STREAMS * 8)
    spans = list(zip(ends[:-1], ends[1:]))
    places = [*reversed(z), *reversed(y), ("slot", 0), *reversed(x)]
    states = [(acc, [], span, list(places)) for span in spans]

    def size_of(items):
        total = 1
        for name, _ in items:
            total *= per_dev if name == "slot" else 2
        return total

    def advance(state, digit):
        kept, come, span, left_over = state
        r = span[1] - span[0]
        inner = span if kept is acc else (0, r)
        at = left_over.index(digit)
        pre, post = size_of(left_over[:at]), size_of(left_over[at + 1 :])
        run = functools.partial(
            half_kernel, span=inner, pre=pre, post=post, axis=digit[0], b=digit[1], ys=ys
        )
        n = pre * post
        (message,) = call(functools.partial(run, send=True), [coded(n, r)], [kept, *come])
        arrived = partner(message, digit[0], 1 << digit[1])
        (keep,) = call(functools.partial(run, send=False), [floats(n, r)], [kept, *come])
        return keep, [arrived], span, left_over[:at] + left_over[at + 1 :]

    for step in range(len(orders[0])):
        states = [advance(state, order[step]) for state, order in zip(states, orders)]

    back = [b for _, b in reversed(low)]
    spot = dict(axis=top[0], b=top[1], ys=ys)
    schur, solved = [], []
    shared = []
    for kept, come, span, _ in states:
        r = span[1] - span[0]
        part, message = call(
            functools.partial(share_kernel, depth=left_depth, span=span, **spot),
            [floats(2 * per_dev, r), coded(2 * per_dev, r)],
            [kept, *come, frontal_tiles],
        )
        shared.append((part, partner(message, top[0], 1 << top[1])))
    for (part, message), span in zip(shared, spans):
        r = span[1] - span[0]
        own, panel = call(
            functools.partial(solve_kernel, **spot),
            [floats(per_dev, r), coded(2 * per_dev, r)],
            [part, message, diag_inverse],
            scratch=[pltpu.VMEM((2 * per_dev, depth, r, columns), jnp.float32)],
        )
        schur.append(own)
        solved.append([panel])
    for b in back:
        for s, parts in enumerate(solved):
            have = parts[0]
            if len(parts) > 1:
                total = sum(p.shape[0] for p in parts)
                (have,) = call(join_kernel, [pltpu.VMEM((total, columns), jnp.int32)], parts)
            solved[s] = [have, partner(have, "z", 1 << b)]
    chosen = dict(ys=ys, top=top[1], bits=back, per_dev=per_dev, reads=reads, depth=depth)
    for s, (parts, span) in enumerate(zip(solved, spans)):
        r = span[1] - span[0]
        picked = call(
            functools.partial(pick_kernel, outs=ys - 1, rows=r, **chosen),
            [coded(reads, r)] * (ys - 1),
            [reader_tile, *parts],
            smem=1,
        )
        solved[s] = parts + [partner(p, "y", j) for j, p in enumerate(picked, 1)]
    (ancestor,) = call(
        functools.partial(schur_kernel, spans=spans),
        [jax.ShapeDtypeStruct((per_dev, depth, rows, columns), jnp.float32)],
        schur,
    )
    out = None
    for parts, span in zip(solved, spans):
        r = span[1] - span[0]
        far = pl.BlockSpec(memory_space=pltpu.HBM)
        before = [] if out is None else [out]
        out = pl.pallas_call(
            functools.partial(read_kernel, span=span, many=len(parts), **chosen),
            out_shape=jax.ShapeDtypeStruct((reads, depth, rows, columns), jnp.float32),
            in_specs=[pl.BlockSpec(memory_space=pltpu.SMEM)]
            + [pl.BlockSpec(memory_space=pltpu.VMEM)] * len(parts)
            + [far] * len(before),
            out_specs=far,
            scratch_shapes=[
                pltpu.VMEM((reads, depth, r, columns), jnp.float32),
                pltpu.SemaphoreType.DMA((reads,)),
            ],
            input_output_aliases={1 + len(parts): 0} if before else {},
            compiler_params=pltpu.CompilerParams(vmem_limit_bytes=4 << 20),
        )(reader_tile, *map(near, parts), *before)
    return ancestor, out


def tile_rows(mesh):
    line = mesh.devices[0]
    places = [getattr(d, "coords", None) for d in line]
    if any(p is None for p in places):
        return mesh.shape["forest"] // CORES
    count = 1
    while count < len(line) and places[count][2] == places[0][2]:
        count += 1
    return count


def solution(mesh):
    placed = (
        P("forest", "tile", None, None, None),
        P("forest", "tile", None, None, None),
        P("forest", "tile", None),
        P("forest", "tile"),
        P("tile", None, "forest", None),
        P(),
        P(),
    )
    return jax.shard_map(
        functools.partial(per_device, ys=tile_rows(mesh)),
        mesh=mesh,
        in_specs=placed,
        out_specs=(P("tile", None, "forest", None), P("tile", None, "forest", None)),
        check_vma=False,
    )
```
